512 devices in a mesh: ctx: 32 (over z_lo, x, core), head: 16 (over y, z_hi).
Axes of the slice: x: 4, y: 4, z: 16 (z_hi: 4, z_lo: 4; z = z_hi * 4 + z_lo), core: 2. Of those that a mesh axis runs over, the one named last changes fastest.
Arguments:
- hidden_in: bfloat16 [4096, 4096], P('ctx', 'head'), may hold values from -6 to 6
- queries: bfloat16 [4096, 4096], P('ctx', 'head'), may hold values from -16 to 16
- kv_prev: bfloat16 [4096, 2, 4096], P('ctx', None, 'head'), may hold values from -16 to 16
- norm_gain: bfloat16 [4096], replicated, may hold values from 0.099609375 to 1.8984375
- w_kv: bfloat16 [4096, 2, 4096], P(None, None, 'head'), may hold values from -0.09375 to 0.09375
- w_out: bfloat16 [4096, 4096], P('head', 'ctx'), may hold values from -0.1875 to 0.1875
Outputs:
- hidden_out: float32 [4096, 4096], P('ctx', 'head')
- kv_out: float32 [4096, 2, 4096], P('ctx', None, 'head')
The draws below stay inside these ranges and needn't reach their ends.
All inputs are finite; a program needn't handle non-finite values.
Results may differ from the reference program's by a relative error of at most 0.033.
Values may be sent and summed in bfloat16 or wider, within the bound.
No kernel may reach another device: no remote copies, remote signals or barrier semaphores. Data moves between devices by JAX's collectives and lax.ppermute only.
A program may use at most 64 MiB of HBM per device.

```python
import jax
import jax.numpy as jnp
from jax import lax

D = 4096
HEADS = 32
HD = 128
ITERS = 2
SEQ = 4096
N_HEAD = 16


def shared_pair(key):
    folded = jax.random.fold_in(key, 1931)
    key_query, key_keys, key_values = jax.random.split(folded, 3)
    query_draw = jnp.clip(jax.random.normal(key_query, (SEQ, D), jnp.float32), -4.0, 4.0)
    key_draw = jnp.clip(jax.random.normal(key_keys, (SEQ, D), jnp.float32), -4.0, 4.0)
    value_draw = jnp.clip(jax.random.normal(key_values, (SEQ, D), jnp.float32), -4.0, 4.0)
    return (query_draw, jnp.stack([key_draw, value_draw], axis=1))


def draw_queries(key, part):
    return shared_pair(key)[0].astype(jnp.bfloat16)


def draw_kv_prev(key, part):
    return shared_pair(key)[1].astype(jnp.bfloat16)


def draw_hidden_in(key, part):
    key_first, key_second = jax.random.split(jax.random.fold_in(key, 577))
    columns = jnp.arange(D).astype(jnp.float32) / D
    drawn = jnp.clip(jax.random.normal(key_first, (SEQ, D), jnp.float32), -4.0, 4.0)
    drawn = drawn * jax.random.uniform(key_second, (SEQ, D), jnp.float32, 0.6, 1.4)
    rising = 0.25 * jnp.exp(jnp.log(3.0) * columns)
    return (drawn * rising[None, :]).astype(jnp.bfloat16)


def block_scale(own_key, dims, pieces, smallest, top_value):
    def one(dim, parts):
        steps = jax.random.uniform(jax.random.fold_in(jax.random.fold_in(own_key, 6), dim), (parts,), jnp.float32, smallest / len(pieces), top_value / len(pieces))
        return jnp.repeat(jnp.exp(steps), dims[dim] // parts).reshape((-1,) + (1,) * (len(dims) - dim - 1))

    loudness = one(*pieces[0])
    for cut in pieces[1:]:
        loudness = loudness * one(*cut)
    return loudness


def scatter_about(stream_key, shape, scale, reach, cuts=(), held_as=jnp.bfloat16):
    gain = block_scale(stream_key, shape, cuts, -0.22, 0.18) if cuts else 1.0
    result = jax.random.normal(stream_key, shape, jnp.float32) * scale * gain
    return jnp.minimum(jnp.maximum(result, -reach), reach).astype(held_as)


def setup_inputs(seed: int = 0) -> dict:
    arg_keys = jax.random.split(jax.random.key(seed), 7)
    hidden_in = draw_hidden_in(jax.random.fold_in(arg_keys[6], 71), 0)
    queries = draw_queries(jax.random.fold_in(arg_keys[6], 71), 0)
    kv_prev = draw_kv_prev(jax.random.fold_in(arg_keys[6], 71), 0)
    norm_gain = jnp.clip(1.0 + 0.18 * jax.random.normal(arg_keys[3], (D,), jnp.float32), 0.099609375, 1.8984375).astype(jnp.bfloat16)
    w_kv = scatter_about(arg_keys[4], (D, 2, D), D ** -0.5, 0.09375, ((2, 16),))
    w_out = scatter_about(arg_keys[5], (D, D), (D // 4) ** -0.5, 0.1875, ((0, 16), (1, 32)))
    return dict(hidden_in=hidden_in, queries=queries, kv_prev=kv_prev, norm_gain=norm_gain, w_kv=w_kv, w_out=w_out)


MASKED = -1e+30
EPSILON = 1e-05

def attend_head(triple):
    query_rows, key_rows, value_rows = triple
    scores = jnp.dot(query_rows, key_rows.T, preferred_element_type=jnp.float32) * HD ** (-0.5)
    positions = jnp.arange(query_rows.shape[0])
    causal = positions[:, None] >= positions[None, :]
    scores = jnp.where(causal, scores, MASKED)
    row_max = lax.optimization_barrier(jnp.max(scores, axis=1, keepdims=True))
    weights = jnp.where(causal, jnp.exp(scores - row_max), 0.0)
    row_sum = lax.optimization_barrier(jnp.sum(weights, axis=1, keepdims=True))
    combined = jnp.dot(weights.astype(jnp.bfloat16), value_rows, preferred_element_type=jnp.float32)
    return (combined / row_sum).astype(jnp.bfloat16)

def split_heads(matrix):
    return matrix.reshape(matrix.shape[0], HEADS, HD).transpose(1, 0, 2)

def attend(queries, key_value):
    length = queries.shape[0]
    outputs = lax.map(attend_head, (split_heads(queries), split_heads(key_value[:, 0]), split_heads(key_value[:, 1])))
    return outputs.transpose(1, 0, 2).reshape(length, HEADS * HD)

def iterate(hidden_in, queries, key_value, norm_gain, w_kv, w_out):
    length = queries.shape[0]
    group_width = D // N_HEAD
    attended = attend(queries, key_value)
    attended_groups = attended.reshape(length, N_HEAD, group_width).transpose(1, 0, 2)
    weight_groups = w_out.reshape(N_HEAD, group_width, D)

    def add_group(running, pair_in):
        group_share = jnp.dot(pair_in[0], pair_in[1], preferred_element_type=jnp.float32)
        group_share = lax.optimization_barrier(group_share.astype(jnp.bfloat16)).astype(jnp.float32)
        return (running + group_share, None)
    branch_sum, unused = lax.scan(add_group, jnp.zeros((length, D), jnp.float32), (attended_groups, weight_groups))
    hidden = hidden_in.astype(jnp.float32) + branch_sum
    mean_square = lax.optimization_barrier(jnp.mean(hidden * hidden, axis=1, keepdims=True))
    normed = (hidden * lax.rsqrt(mean_square + EPSILON) * norm_gain.astype(jnp.float32)).astype(jnp.bfloat16)
    kv_product = jnp.dot(normed, w_kv.reshape(D, 2 * D), preferred_element_type=jnp.float32).reshape(length, 2, D)
    return (hidden, kv_product)

def reference(hidden_in, queries, kv_prev, norm_gain, w_kv, w_out):
    key_value = kv_prev
    for iteration in range(ITERS):
        hidden_out, kv_product = iterate(hidden_in, queries, key_value, norm_gain, w_kv, w_out)
        key_value = kv_product.astype(jnp.bfloat16)
    return (hidden_out, kv_product)
```

```python
import jax
import jax.numpy as jnp
from jax import lax
from jax.experimental import pallas as pl
from jax.experimental.pallas import tpu as pltpu
from jax.sharding import Mesh, PartitionSpec as P

D = 4096
HD = 128
ITERS = 2

MASKED = -1e30
EPSILON = 1e-05

CTX = ("zl", "x", "co")
HEAD = ("y", "zh")
VMEM_LIMIT = 56 << 20


def spread(block, axis, count):
    copies = jnp.broadcast_to(block[None], (count,) + block.shape)
    return lax.all_to_all(copies, axis, 0, 0, tiled=True)


def attend_kernel(place_ref, q_ref, own_ref, other_ref, out_ref, m_ref, l_ref, acc_ref):
    zl = place_ref[0]
    x = place_ref[1]
    co = place_ref[2]
    rows = q_ref.shape[0]
    heads = q_ref.shape[1] // HD
    scale = HD ** (-0.5)
    row_position = zl * 1024 + x * 256 + co * 128 + lax.broadcasted_iota(jnp.int32, (rows, 128), 0)
    lane = lax.broadcasted_iota(jnp.int32, (rows, 128), 1)

    for chunk in range(4):

        @pl.when(chunk <= zl)
        def _(chunk=chunk):
            base = chunk * 1024 + lane
            allowed = jnp.concatenate(
                [row_position >= base + xx * 256 + co * 128 for xx in range(4)]
                + [row_position >= base + xx * 256 + (1 - co) * 128 for xx in range(4)],
                axis=1,
            )
            for head in range(heads):
                cols = slice(head * HD, (head + 1) * HD)
                keys = jnp.concatenate(
                    [ref[xx, chunk, 0, :, cols] for ref in (own_ref, other_ref) for xx in range(4)], axis=0
                )
                values = jnp.concatenate(
                    [ref[xx, chunk, 1, :, cols] for ref in (own_ref, other_ref) for xx in range(4)], axis=0
                )
                scores = (
                    lax.dot_general(
                        q_ref[:, cols], keys, (((1,), (1,)), ((), ())), preferred_element_type=jnp.float32
                    )
                    * scale
                )
                scores = jnp.where(allowed, scores, MASKED)
                top = jnp.max(scores, axis=1, keepdims=True)
                if chunk == 0:
                    weights = jnp.exp(scores - top)
                    m_ref[head] = jnp.broadcast_to(top, (rows, 128))
                    l_ref[head] = jnp.broadcast_to(jnp.sum(weights, axis=1, keepdims=True), (rows, 128))
                    acc_ref[head] = jnp.dot(
                        weights.astype(jnp.bfloat16), values, preferred_element_type=jnp.float32
                    )
                else:
                    before = m_ref[head]
                    now = jnp.maximum(before, top)
                    fade = jnp.exp(before - now)
                    weights = jnp.exp(scores - now[:, :1])
                    m_ref[head] = now
                    l_ref[head] = l_ref[head] * fade + jnp.sum(weights, axis=1, keepdims=True)
                    acc_ref[head] = acc_ref[head] * fade + jnp.dot(
                        weights.astype(jnp.bfloat16), values, preferred_element_type=jnp.float32
                    )

    for head in range(heads):
        cols = slice(head * HD, (head + 1) * HD)
        result = (acc_ref[head] / l_ref[head]).astype(jnp.bfloat16)
        for copy in range(4):
            out_ref[copy, :, cols] = result


def attend(place, queries, own, other):
    rows, width = queries.shape
    heads = width // HD
    return pl.pallas_call(
        attend_kernel,
        out_shape=jax.ShapeDtypeStruct((4, rows, width), jnp.bfloat16),
        in_specs=[pl.BlockSpec(memory_space=pltpu.SMEM)] + [pl.BlockSpec(memory_space=pltpu.VMEM)] * 3,
        out_specs=pl.BlockSpec(memory_space=pltpu.VMEM),
        scratch_shapes=[pltpu.VMEM((heads, rows, 128), jnp.float32)] * 2
        + [pltpu.VMEM((heads, rows, HD), jnp.float32)],
        compiler_params=pltpu.CompilerParams(vmem_limit_bytes=VMEM_LIMIT),
        name="attend",
    )(place, queries, own, other)


def project_out_kernel(att_ref, w_ref, in_ref, sent_ref, hidden_ref=None):
    groups, rows, width = att_ref.shape
    total = in_ref[...].astype(jnp.float32)
    branch = jnp.zeros_like(total)
    for group in range(groups):
        branch = branch + jnp.dot(
            att_ref[group], w_ref[group * width : (group + 1) * width, :], preferred_element_type=jnp.float32
        )
    hidden = total + branch
    if hidden_ref is not None:
        hidden_ref[...] = hidden
    sent = hidden.astype(jnp.bfloat16)
    for copy in range(4):
        sent_ref[copy] = sent


def project_out(gathered, w_cols, hidden_in, last):
    groups, rows, width = gathered.shape
    shapes = [jax.ShapeDtypeStruct((4, rows, width), jnp.bfloat16)]
    if last:
        shapes.append(jax.ShapeDtypeStruct((rows, width), jnp.float32))
    return pl.pallas_call(
        project_out_kernel,
        out_shape=shapes,
        in_specs=[pl.BlockSpec(memory_space=pltpu.VMEM)] * 3,
        out_specs=[pl.BlockSpec(memory_space=pltpu.VMEM)] * len(shapes),
        compiler_params=pltpu.CompilerParams(vmem_limit_bytes=VMEM_LIMIT),
        name="project_out",
    )(gathered, w_cols, hidden_in)


def project_kv_kernel(hid_ref, gain_ref, w_ref, out_ref):
    groups, rows, width = hid_ref.shape
    squares = jnp.zeros((rows, width), jnp.float32)
    keys = jnp.zeros((rows, width), jnp.float32)
    values = jnp.zeros((rows, width), jnp.float32)
    for group in range(groups):
        hidden = hid_ref[group].astype(jnp.float32)
        squares = squares + hidden * hidden
        scaled = (hidden * gain_ref[group : group + 1, :].astype(jnp.float32)).astype(jnp.bfloat16)
        span = slice(group * width, (group + 1) * width)
        keys = keys + jnp.dot(scaled, w_ref[0, span, :], preferred_element_type=jnp.float32)
        values = values + jnp.dot(scaled, w_ref[1, span, :], preferred_element_type=jnp.float32)
    norm = lax.rsqrt(jnp.sum(squares, axis=1, keepdims=True) / D + EPSILON)
    if len(out_ref.shape) == 4:
        for copy in range(4):
            out_ref[copy, 0] = (keys * norm).astype(out_ref.dtype)
            out_ref[copy, 1] = (values * norm).astype(out_ref.dtype)
    else:
        out_ref[0] = keys * norm
        out_ref[1] = values * norm


def project_kv(gathered, gain, w_kv, last):
    groups, rows, width = gathered.shape
    if last:
        shape = jax.ShapeDtypeStruct((2, rows, width), jnp.float32)
    else:
        shape = jax.ShapeDtypeStruct((4, 2, rows, width), jnp.bfloat16)
    return pl.pallas_call(
        project_kv_kernel,
        out_shape=shape,
        in_specs=[pl.BlockSpec(memory_space=pltpu.VMEM)] * 3,
        out_specs=pl.BlockSpec(memory_space=pltpu.VMEM),
        compiler_params=pltpu.CompilerParams(vmem_limit_bytes=VMEM_LIMIT),
        name="project_kv",
    )(gathered, gain, w_kv)


def exchange(copies, axis):
    return lax.all_to_all(copies, axis, 0, 0, tiled=True)


def over_head(copies):
    near = exchange(copies, "zh")
    far = spread(near, "y", 4)
    return far.reshape((16,) + copies.shape[1:])


def redistribute(w_out):
    half = w_out.shape[0] // 2
    parity = lax.axis_index("co")
    first = lax.dynamic_slice_in_dim(w_out, parity * half, half, 0)
    second = lax.dynamic_slice_in_dim(w_out, (1 - parity) * half, half, 0)
    axes = CTX + HEAD
    same, cross = [], []
    for c in range(32):
        for h in range(16):
            same.append((c * 16 + h, (2 * h + c % 2) * 16 + c // 2))
            cross.append((c * 16 + h, (2 * h + 1 - c % 2) * 16 + c // 2))
    got_same = lax.ppermute(first, axes, same)
    got_cross = lax.ppermute(second, axes, cross)
    low = jnp.where(parity == 0, got_same, got_cross)
    high = jnp.where(parity == 0, got_cross, got_same)
    mine = jnp.concatenate([low, high], axis=1)
    return lax.all_gather(mine, CTX, axis=0, tiled=True)


def per_device(hidden_in, queries, kv_prev, norm_gain, w_kv, w_out):
    place = jnp.stack([lax.axis_index("zl"), lax.axis_index("x"), lax.axis_index("co")]).astype(jnp.int32)
    w_cols = redistribute(w_out)
    w_pair = jnp.transpose(w_kv, (1, 0, 2))
    gain = norm_gain.reshape(16, 256)
    pair = jnp.transpose(kv_prev, (1, 0, 2))
    copies = jnp.broadcast_to(pair[None], (4,) + pair.shape)
    for iteration in range(ITERS):
        last = iteration == ITERS - 1
        own = spread(exchange(copies, "zl"), "x", 4)
        other = lax.ppermute(own, "co", [(0, 1), (1, 0)])
        attended = attend(place, queries, own, other)
        projected = project_out(over_head(attended), w_cols, hidden_in, last)
        copies = project_kv(over_head(projected[0]), gain, w_pair, last)
    return (projected[1], jnp.transpose(copies, (1, 0, 2)))


def solution(mesh):
    ctx_parts = (4, 4, 2)
    head_parts = (4, 4)
    fine = Mesh(mesh.devices.reshape(ctx_parts + head_parts), CTX + HEAD)
    in_specs = (
        P(CTX, HEAD),
        P(CTX, HEAD),
        P(CTX, None, HEAD),
        P(),
        P(None, None, HEAD),
        P(HEAD, CTX),
    )
    out_specs = (P(CTX, HEAD), P(CTX, None, HEAD))
    return jax.shard_map(per_device, mesh=fine, in_specs=in_specs, out_specs=out_specs, check_vma=False)
```

```python
import jax
import jax.numpy as jnp
from jax import lax
from jax.experimental import pallas as pl
from jax.experimental.pallas import tpu as pltpu
from jax.sharding import Mesh, PartitionSpec as P

D = 4096
HD = 128
ITERS = 2

MASKED = -1e30
EPSILON = 1e-05

CTX = ("zl", "x", "co")
HEAD = ("y", "zh")
VMEM_LIMIT = 56 << 20


def spread(block, axis, count):
    copies = jnp.broadcast_to(block[None], (count,) + block.shape)
    return lax.all_to_all(copies, axis, 0, 0, tiled=True)


def attend_kernel(
    place_ref, q_ref, own_ref, other_ref, w_own_ref, w_other_ref, out_ref, m_ref, l_ref, acc_ref
):
    zl = place_ref[0]
    x = place_ref[1]
    co = place_ref[2]
    rows = q_ref.shape[0]
    heads = q_ref.shape[1] // HD
    scale = HD ** (-0.5)
    row_position = zl * 1024 + x * 256 + co * 128 + lax.broadcasted_iota(jnp.int32, (rows, 128), 0)
    lane = lax.broadcasted_iota(jnp.int32, (rows, 128), 1)

    for chunk in range(4):

        @pl.when(chunk <= zl)
        def _(chunk=chunk):
            base = chunk * 1024 + lane
            allowed = jnp.concatenate(
                [row_position >= base + xx * 256 + co * 128 for xx in range(4)]
                + [row_position >= base + xx * 256 + (1 - co) * 128 for xx in range(4)],
                axis=1,
            )
            for head in range(heads):
                cols = slice(head * HD, (head + 1) * HD)
                keys = jnp.concatenate(
                    [ref[xx, chunk, 0, :, cols] for ref in (own_ref, other_ref) for xx in range(4)], axis=0
                )
                values = jnp.concatenate(
                    [ref[xx, chunk, 1, :, cols] for ref in (own_ref, other_ref) for xx in range(4)], axis=0
                )
                scores = (
                    lax.dot_general(
                        q_ref[:, cols], keys, (((1,), (1,)), ((), ())), preferred_element_type=jnp.float32
                    )
                    * scale
                )
                scores = jnp.where(allowed, scores, MASKED)
                top = jnp.max(scores, axis=1, keepdims=True)
                if chunk == 0:
                    weights = jnp.exp(scores - top)
                    m_ref[head] = jnp.broadcast_to(top, (rows, 128))
                    l_ref[head] = jnp.broadcast_to(jnp.sum(weights, axis=1, keepdims=True), (rows, 128))
                    acc_ref[head] = jnp.dot(
                        weights.astype(jnp.bfloat16), values, preferred_element_type=jnp.float32
                    )
                else:
                    before = m_ref[head]
                    now = jnp.maximum(before, top)
                    fade = jnp.exp(before - now)
                    weights = jnp.exp(scores - now[:, :1])
                    m_ref[head] = now
                    l_ref[head] = l_ref[head] * fade + jnp.sum(weights, axis=1, keepdims=True)
                    acc_ref[head] = acc_ref[head] * fade + jnp.dot(
                        weights.astype(jnp.bfloat16), values, preferred_element_type=jnp.float32
                    )

    attended = jnp.concatenate(
        [(acc_ref[head] / l_ref[head]).astype(jnp.bfloat16) for head in range(heads)], axis=1
    )
    for y in range(4):
        for zh in range(4):
            block = jnp.concatenate(
                [
                    jnp.concatenate([ref[zh, y, 0, :, :128], ref[zh, y, 0, :, 128:]], axis=0)
                    for ref in (w_own_ref, w_other_ref)
                ],
                axis=1,
            )
            product = jnp.dot(attended, block, preferred_element_type=jnp.float32)
            mine, theirs = product[:, :128], product[:, 128:]
            out_ref[y, zh, :, :128] = jnp.where(co == 0, mine, theirs).astype(jnp.bfloat16)
            out_ref[y, zh, :, 128:] = jnp.where(co == 0, theirs, mine).astype(jnp.bfloat16)


def whole(shape):
    return pl.BlockSpec(shape, lambda step: (0,) * len(shape))


def attend(place, queries, own, other, w_own, w_other):
    rows, width = queries.shape
    heads = width // HD
    pair = (4, 4, 2, 128, width)
    plane = pl.BlockSpec((4, 4, 1, 128, width), lambda step: (0, 0, 2, 0, 0))
    return pl.pallas_call(
        attend_kernel,
        out_shape=jax.ShapeDtypeStruct((4, 4, rows, width), jnp.bfloat16),
        grid=(1,),
        in_specs=[
            pl.BlockSpec(memory_space=pltpu.SMEM),
            whole((rows, width)),
            whole(pair),
            whole(pair),
            plane,
            plane,
        ],
        out_specs=whole((4, 4, rows, width)),
        scratch_shapes=[pltpu.VMEM((heads, rows, 128), jnp.float32)] * 2
        + [pltpu.VMEM((heads, rows, HD), jnp.float32)],
        compiler_params=pltpu.CompilerParams(vmem_limit_bytes=VMEM_LIMIT),
        name="attend",
    )(place, queries, own, other, w_own, w_other)


def finish_hidden_kernel(parts_ref, in_ref, sent_ref, hidden_ref=None):
    hidden = in_ref[...].astype(jnp.float32)
    for part in range(parts_ref.shape[0]):
        hidden = hidden + parts_ref[part].astype(jnp.float32)
    if hidden_ref is not None:
        hidden_ref[...] = hidden
    sent = hidden.astype(jnp.bfloat16)
    for copy in range(4):
        sent_ref[copy] = sent


def finish_hidden(parts, hidden_in, last):
    count, rows, width = parts.shape
    shapes = [jax.ShapeDtypeStruct((4, rows, width), jnp.bfloat16)]
    if last:
        shapes.append(jax.ShapeDtypeStruct((rows, width), jnp.float32))
    return pl.pallas_call(
        finish_hidden_kernel,
        out_shape=shapes,
        in_specs=[pl.BlockSpec(memory_space=pltpu.VMEM)] * 2,
        out_specs=[pl.BlockSpec(memory_space=pltpu.VMEM)] * len(shapes),
        compiler_params=pltpu.CompilerParams(vmem_limit_bytes=VMEM_LIMIT),
        name="finish_hidden",
    )(parts, hidden_in)


def project_kv_kernel(hid_ref, gain_ref, w_ref, out_ref):
    groups, rows, width = hid_ref.shape
    squares = jnp.zeros((rows, width), jnp.float32)
    keys = jnp.zeros((rows, width), jnp.float32)
    values = jnp.zeros((rows, width), jnp.float32)
    for group in range(groups):
        hidden = hid_ref[group].astype(jnp.float32)
        squares = squares + hidden * hidden
        scaled = (hidden * gain_ref[group : group + 1, :].astype(jnp.float32)).astype(jnp.bfloat16)
        span = slice(group * width, (group + 1) * width)
        keys = keys + jnp.dot(scaled, w_ref[0, span, :], preferred_element_type=jnp.float32)
        values = values + jnp.dot(scaled, w_ref[1, span, :], preferred_element_type=jnp.float32)
    norm = lax.rsqrt(jnp.sum(squares, axis=1, keepdims=True) / D + EPSILON)
    if len(out_ref.shape) == 4:
        for copy in range(4):
            out_ref[copy, 0] = (keys * norm).astype(out_ref.dtype)
            out_ref[copy, 1] = (values * norm).astype(out_ref.dtype)
    else:
        out_ref[0] = keys * norm
        out_ref[1] = values * norm


def project_kv(gathered, gain, w_kv, last):
    groups, rows, width = gathered.shape
    if last:
        shape = jax.ShapeDtypeStruct((2, rows, width), jnp.float32)
    else:
        shape = jax.ShapeDtypeStruct((4, 2, rows, width), jnp.bfloat16)
    return pl.pallas_call(
        project_kv_kernel,
        out_shape=shape,
        in_specs=[pl.BlockSpec(memory_space=pltpu.VMEM)] * 3,
        out_specs=pl.BlockSpec(memory_space=pltpu.VMEM),
        compiler_params=pltpu.CompilerParams(vmem_limit_bytes=VMEM_LIMIT),
        name="project_kv",
    )(gathered, gain, w_kv)


def exchange(copies, axis):
    return lax.all_to_all(copies, axis, 0, 0, tiled=True)


def over_head(copies):
    near = exchange(copies, "zh")
    far = spread(near, "y", 4)
    return far.reshape((16,) + copies.shape[1:])


def per_device(hidden_in, queries, kv_prev, norm_gain, w_kv, w_out):
    place = jnp.stack([lax.axis_index("zl"), lax.axis_index("x"), lax.axis_index("co")]).astype(jnp.int32)
    w_pair = jnp.transpose(w_kv, (1, 0, 2))
    gain = norm_gain.reshape(16, 256)
    half = w_out.shape[0] // 2
    w_packed = jnp.concatenate([w_out[:half], w_out[half:]], axis=1)
    block = jnp.concatenate([jnp.transpose(kv_prev, (1, 0, 2)), w_packed[None]], axis=0)
    copies = jnp.broadcast_to(block[None], (4,) + block.shape)
    for iteration in range(ITERS):
        last = iteration == ITERS - 1
        own = spread(exchange(copies, "zl"), "x", 4)
        other = lax.ppermute(own, "co", [(0, 1), (1, 0)])
        if iteration == 0:
            w_own, w_other = own, other
        partial = exchange(attend(place, queries, own, other, w_own, w_other), "y")
        summed = jnp.sum(partial.astype(jnp.float32), axis=0).astype(jnp.bfloat16)
        finished = finish_hidden(exchange(summed, "zh"), hidden_in, last)
        copies = project_kv(over_head(finished[0]), gain, w_pair, last)
    return (finished[1], jnp.transpose(copies, (1, 0, 2)))


def solution(mesh):
    ctx_parts = (4, 4, 2)
    head_parts = (4, 4)
    fine = Mesh(mesh.devices.reshape(ctx_parts + head_parts), CTX + HEAD)
    in_specs = (
        P(CTX, HEAD),
        P(CTX, HEAD),
        P(CTX, None, HEAD),
        P(),
        P(None, None, HEAD),
        P(HEAD, CTX),
    )
    out_specs = (P(CTX, HEAD), P(CTX, None, HEAD))
    return jax.shard_map(per_device, mesh=fine, in_specs=in_specs, out_specs=out_specs, check_vma=False)
```

```python
import jax
import jax.numpy as jnp
from jax import lax
from jax.experimental import pallas as pl
from jax.experimental.pallas import tpu as pltpu
from jax.sharding import Mesh, PartitionSpec as P

D = 4096
HD = 128
ITERS = 2

MASKED = -1e30
EPSILON = 1e-05

CTX = ("zl", "x", "co")
HEAD = ("y", "zh")
VMEM_LIMIT = 56 << 20


def spread(block, axis, count):
    copies = jnp.broadcast_to(block[None], (count,) + block.shape)
    return lax.all_to_all(copies, axis, 0, 0, tiled=True)


def attend_kernel(place_ref, q_ref, own_ref, other_ref, out_ref, m_ref, l_ref, acc_ref):
    zl = place_ref[0]
    x = place_ref[1]
    co = place_ref[2]
    rows = q_ref.shape[0]
    heads = q_ref.shape[1] // HD
    scale = HD ** (-0.5)
    row_position = zl * 1024 + x * 256 + co * 128 + lax.broadcasted_iota(jnp.int32, (rows, 128), 0)
    lane = lax.broadcasted_iota(jnp.int32, (rows, 128), 1)

    for chunk in range(4):

        @pl.when(chunk <= zl)
        def _(chunk=chunk):
            base = chunk * 1024 + lane
            allowed = jnp.concatenate(
                [row_position >= base + xx * 256 + co * 128 for xx in range(4)]
                + [row_position >= base + xx * 256 + (1 - co) * 128 for xx in range(4)],
                axis=1,
            )
            for head in range(heads):
                cols = slice(head * HD, (head + 1) * HD)
                keys = jnp.concatenate(
                    [ref[xx, chunk, 0, :, cols] for ref in (own_ref, other_ref) for xx in range(4)], axis=0
                )
                values = jnp.concatenate(
                    [ref[xx, chunk, 1, :, cols] for ref in (own_ref, other_ref) for xx in range(4)], axis=0
                )
                scores = (
                    lax.dot_general(
                        q_ref[:, cols], keys, (((1,), (1,)), ((), ())), preferred_element_type=jnp.float32
                    )
                    * scale
                )
                scores = jnp.where(allowed, scores, MASKED)
                top = jnp.max(scores, axis=1, keepdims=True)
                if chunk == 0:
                    weights = jnp.exp(scores - top)
                    m_ref[head] = jnp.broadcast_to(top, (rows, 128))
                    l_ref[head] = jnp.broadcast_to(jnp.sum(weights, axis=1, keepdims=True), (rows, 128))
                    acc_ref[head] = jnp.dot(
                        weights.astype(jnp.bfloat16), values, preferred_element_type=jnp.float32
                    )
                else:
                    before = m_ref[head]
                    now = jnp.maximum(before, top)
                    fade = jnp.exp(before - now)
                    weights = jnp.exp(scores - now[:, :1])
                    m_ref[head] = now
                    l_ref[head] = l_ref[head] * fade + jnp.sum(weights, axis=1, keepdims=True)
                    acc_ref[head] = acc_ref[head] * fade + jnp.dot(
                        weights.astype(jnp.bfloat16), values, preferred_element_type=jnp.float32
                    )

    for head in range(heads):
        cols = slice(head * HD, (head + 1) * HD)
        result = (acc_ref[head] / l_ref[head]).astype(jnp.bfloat16)
        for copy in range(4):
            out_ref[copy, :, cols] = result


def whole(shape):
    return pl.BlockSpec(shape, lambda step: (0,) * len(shape))


def attend(place, queries, own, other):
    rows, width = queries.shape
    heads = width // HD
    pair = (4, 4, 2, 128, width)
    return pl.pallas_call(
        attend_kernel,
        out_shape=jax.ShapeDtypeStruct((4, rows, width), jnp.bfloat16),
        grid=(1,),
        in_specs=[pl.BlockSpec(memory_space=pltpu.SMEM), whole((rows, width)), whole(pair), whole(pair)],
        out_specs=whole((4, rows, width)),
        scratch_shapes=[pltpu.VMEM((heads, rows, 128), jnp.float32)] * 2
        + [pltpu.VMEM((heads, rows, HD), jnp.float32)],
        compiler_params=pltpu.CompilerParams(vmem_limit_bytes=VMEM_LIMIT),
        name="attend",
    )(place, queries, own, other)


def project_out_kernel(place_ref, att_ref, w_own_ref, w_other_ref, out_ref):
    co = place_ref[2]
    for zh in range(4):
        product = None
        for y in range(4):
            block = jnp.concatenate(
                [
                    jnp.concatenate([ref[zh, y, 0, :, :128], ref[zh, y, 0, :, 128:]], axis=0)
                    for ref in (w_own_ref, w_other_ref)
                ],
                axis=1,
            )
            term = jnp.dot(att_ref[y], block, preferred_element_type=jnp.float32)
            product = term if product is None else product + term
        mine, theirs = product[:, :128], product[:, 128:]
        out_ref[zh, :, :128] = jnp.where(co == 0, mine, theirs).astype(jnp.bfloat16)
        out_ref[zh, :, 128:] = jnp.where(co == 0, theirs, mine).astype(jnp.bfloat16)


def project_out(place, attended, w_own, w_other):
    count, rows, width = attended.shape
    plane = pl.BlockSpec((4, 4, 1, 128, width), lambda step: (0, 0, 2, 0, 0))
    return pl.pallas_call(
        project_out_kernel,
        out_shape=jax.ShapeDtypeStruct((4, rows, width), jnp.bfloat16),
        grid=(1,),
        in_specs=[pl.BlockSpec(memory_space=pltpu.SMEM), whole((count, rows, width)), plane, plane],
        out_specs=whole((4, rows, width)),
        compiler_params=pltpu.CompilerParams(vmem_limit_bytes=VMEM_LIMIT),
        name="project_out",
    )(place, attended, w_own, w_other)


def finish_hidden_kernel(parts_ref, in_ref, sent_ref, hidden_ref=None):
    hidden = in_ref[...].astype(jnp.float32)
    for part in range(parts_ref.shape[0]):
        hidden = hidden + parts_ref[part].astype(jnp.float32)
    if hidden_ref is not None:
        hidden_ref[...] = hidden
    sent_ref[...] = hidden.astype(jnp.bfloat16)


def finish_hidden(parts, hidden_in, last):
    count, rows, width = parts.shape
    shapes = [jax.ShapeDtypeStruct((rows, width), jnp.bfloat16)]
    if last:
        shapes.append(jax.ShapeDtypeStruct((rows, width), jnp.float32))
    return pl.pallas_call(
        finish_hidden_kernel,
        out_shape=shapes,
        in_specs=[pl.BlockSpec(memory_space=pltpu.VMEM)] * 2,
        out_specs=[pl.BlockSpec(memory_space=pltpu.VMEM)] * len(shapes),
        compiler_params=pltpu.CompilerParams(vmem_limit_bytes=VMEM_LIMIT),
        name="finish_hidden",
    )(parts, hidden_in)


def project_kv_kernel(hid_ref, gain_ref, w_ref, out_ref):
    groups, rows, width = hid_ref.shape
    squares = jnp.zeros((rows, width), jnp.float32)
    keys = jnp.zeros((rows, width), jnp.float32)
    values = jnp.zeros((rows, width), jnp.float32)
    for group in range(groups):
        hidden = hid_ref[group].astype(jnp.float32)
        squares = squares + hidden * hidden
        scaled = (hidden * gain_ref[group : group + 1, :].astype(jnp.float32)).astype(jnp.bfloat16)
        span = slice(group * width, (group + 1) * width)
        keys = keys + jnp.dot(scaled, w_ref[0, span, :], preferred_element_type=jnp.float32)
        values = values + jnp.dot(scaled, w_ref[1, span, :], preferred_element_type=jnp.float32)
    norm = lax.rsqrt(jnp.sum(squares, axis=1, keepdims=True) / D + EPSILON)
    out_ref[0] = (keys * norm).astype(out_ref.dtype)
    out_ref[1] = (values * norm).astype(out_ref.dtype)


def project_kv(gathered, gain, w_kv, last):
    groups, rows, width = gathered.shape
    shape = jax.ShapeDtypeStruct((2, rows, width), jnp.float32 if last else jnp.bfloat16)
    return pl.pallas_call(
        project_kv_kernel,
        out_shape=shape,
        in_specs=[pl.BlockSpec(memory_space=pltpu.VMEM)] * 3,
        out_specs=pl.BlockSpec(memory_space=pltpu.VMEM),
        compiler_params=pltpu.CompilerParams(vmem_limit_bytes=VMEM_LIMIT),
        name="project_kv",
    )(gathered, gain, w_kv)


def exchange(copies, axis):
    return lax.all_to_all(copies, axis, 0, 0, tiled=True)


def over_head(block):
    near = lax.all_gather(block, "zh", axis=0)
    return spread(near, "y", 4).reshape((16,) + block.shape)


def per_device(hidden_in, queries, kv_prev, norm_gain, w_kv, w_out):
    place = jnp.stack([lax.axis_index("zl"), lax.axis_index("x"), lax.axis_index("co")]).astype(jnp.int32)
    w_pair = jnp.transpose(w_kv, (1, 0, 2))
    gain = norm_gain.reshape(16, 256)
    half = w_out.shape[0] // 2
    swap = [(zl * 4 + y, y * 4 + zl) for zl in range(4) for y in range(4)]
    w_mine = lax.ppermute(w_out, ("zl", "y"), swap)
    w_packed = jnp.concatenate([w_mine[:half], w_mine[half:]], axis=1)
    block = jnp.concatenate([jnp.transpose(kv_prev, (1, 0, 2)), w_packed[None]], axis=0)
    for iteration in range(ITERS):
        last = iteration == ITERS - 1
        own = spread(lax.all_gather(block, "zl", axis=0), "x", 4)
        other = lax.ppermute(own, "co", [(0, 1), (1, 0)])
        if iteration == 0:
            w_own, w_other = own, other
        attended = exchange(attend(place, queries, own, other), "y")
        parts = exchange(project_out(place, attended, w_own, w_other), "zh")
        finished = finish_hidden(parts, hidden_in, last)
        block = project_kv(over_head(finished[0]), gain, w_pair, last)
    return (finished[1], jnp.transpose(block, (1, 0, 2)))


def solution(mesh):
    ctx_parts = (4, 4, 2)
    head_parts = (4, 4)
    fine = Mesh(mesh.devices.reshape(ctx_parts + head_parts), CTX + HEAD)
    in_specs = (
        P(CTX, HEAD),
        P(CTX, HEAD),
        P(CTX, None, HEAD),
        P(),
        P(None, None, HEAD),
        P(HEAD, CTX),
    )
    out_specs = (P(CTX, HEAD), P(CTX, None, HEAD))
    return jax.shard_map(per_device, mesh=fine, in_specs=in_specs, out_specs=out_specs, check_vma=False)
```

```python
import functools

import jax
import jax.numpy as jnp
from jax import lax
from jax.experimental import pallas as pl
from jax.experimental.pallas import tpu as pltpu
from jax.sharding import Mesh, PartitionSpec as P


D = 4096
HD = 128
ITERS = 2

MASKED = -1e30
EPSILON = 1e-05

CTX = ("zl", "x", "co")
HEAD = ("y", "zh")
VMEM_LIMIT = 56 << 20


def spread(block, axis, count):
    copies = jnp.broadcast_to(block[None], (count,) + block.shape)
    return lax.all_to_all(copies, axis, 0, 0, tiled=True)


def in_vmem(*arrays):
    return [pltpu.with_memory_space_constraint(array, pltpu.VMEM) for array in arrays]


def vmem_out(shape, dtype):
    return pltpu.VMEM(shape, dtype)


IN_VMEM = pl.BlockSpec(memory_space=pltpu.VMEM)
IN_SMEM = pl.BlockSpec(memory_space=pltpu.SMEM)


def attend_kernel(place_ref, q_ref, kv_ref, *refs, first):
    if first:
        m_ref, l_ref, acc_ref = refs
    else:
        m_in, l_in, acc_in, out_ref, m_ref, l_ref, acc_ref = refs
    zl = place_ref[0]
    x = place_ref[1]
    co = place_ref[2]
    rows = q_ref.shape[0]
    heads = q_ref.shape[1] // HD
    scale = HD ** (-0.5)
    row_position = zl * 1024 + x * 256 + co * 128 + lax.broadcasted_iota(jnp.int32, (rows, 128), 0)
    lane = lax.broadcasted_iota(jnp.int32, (rows, 128), 1)
    side = co if first else 1 - co
    if not first:
        m_ref[...] = m_in[...]
        l_ref[...] = l_in[...]
        acc_ref[...] = acc_in[...]

    for chunk in range(4):

        @pl.when(chunk <= zl)
        def _(chunk=chunk):
            base = chunk * 1024 + side * 128 + lane
            allowed = jnp.concatenate([row_position >= base + xx * 256 for xx in range(4)], axis=1)
            for head in range(heads):
                cols = slice(head * HD, (head + 1) * HD)
                keys = jnp.concatenate([kv_ref[xx, chunk, 0, :, cols] for xx in range(4)], axis=0)
                values = jnp.concatenate([kv_ref[xx, chunk, 1, :, cols] for xx in range(4)], axis=0)
                scores = (
                    lax.dot_general(
                        q_ref[:, cols], keys, (((1,), (1,)), ((), ())), preferred_element_type=jnp.float32
                    )
                    * scale
                )
                scores = jnp.where(allowed, scores, MASKED)
                top = jnp.max(scores, axis=1, keepdims=True)
                if first and chunk == 0:
                    weights = jnp.where(allowed, jnp.exp(scores - top), 0.0)
                    m_ref[head] = jnp.broadcast_to(top, (rows, 128))
                    l_ref[head] = jnp.broadcast_to(jnp.sum(weights, axis=1, keepdims=True), (rows, 128))
                    acc_ref[head] = jnp.dot(
                        weights.astype(jnp.bfloat16), values, preferred_element_type=jnp.float32
                    )
                else:
                    before = m_ref[head]
                    now = jnp.maximum(before, top)
                    fade = jnp.exp(before - now)
                    weights = jnp.where(allowed, jnp.exp(scores - now[:, :1]), 0.0)
                    m_ref[head] = now
                    l_ref[head] = l_ref[head] * fade + jnp.sum(weights, axis=1, keepdims=True)
                    acc_ref[head] = acc_ref[head] * fade + jnp.dot(
                        weights.astype(jnp.bfloat16), values, preferred_element_type=jnp.float32
                    )

    if not first:
        for head in range(heads):
            cols = slice(head * HD, (head + 1) * HD)
            result = (acc_ref[head] / l_ref[head]).astype(jnp.bfloat16)
            for copy in range(4):
                out_ref[copy, :, cols] = result


def attend(place, queries, pair, state=None):
    rows, width = queries.shape
    heads = width // HD
    kept = (heads, rows, 128)
    first = state is None
    if first:
        out_shape = [vmem_out(kept, jnp.float32)] * 3
        operands = in_vmem(queries, pair)
        scratch = []
    else:
        out_shape = vmem_out((4, rows, width), jnp.bfloat16)
        operands = in_vmem(queries) + [pair] + in_vmem(*state)
        scratch = [pltpu.VMEM(kept, jnp.float32)] * 3
    return pl.pallas_call(
        functools.partial(attend_kernel, first=first),
        out_shape=out_shape,
        in_specs=[IN_SMEM] + [IN_VMEM] * len(operands),
        out_specs=[IN_VMEM] * 3 if first else IN_VMEM,
        scratch_shapes=scratch,
        compiler_params=pltpu.CompilerParams(vmem_limit_bytes=VMEM_LIMIT),
        name="attend_own" if first else "attend_other",
    )(place, *operands)


def project_out_kernel(place_ref, att_ref, w_own_ref, w_other_ref, out_ref):
    co = place_ref[2]
    for zh in range(4):
        product = None
        for y in range(4):
            block = jnp.concatenate(
                [
                    jnp.concatenate([ref[zh, y, :, :128], ref[zh, y, :, 128:]], axis=0)
                    for ref in (w_own_ref, w_other_ref)
                ],
                axis=1,
            )
            term = jnp.dot(att_ref[y], block, preferred_element_type=jnp.float32)
            product = term if product is None else product + term
        mine, theirs = product[:, :128], product[:, 128:]
        out_ref[zh, :, :128] = jnp.where(co == 0, mine, theirs).astype(jnp.bfloat16)
        out_ref[zh, :, 128:] = jnp.where(co == 0, theirs, mine).astype(jnp.bfloat16)


def project_out(place, attended, w_own, w_other):
    _, rows, width = attended.shape
    return pl.pallas_call(
        project_out_kernel,
        out_shape=vmem_out((4, rows, width), jnp.bfloat16),
        in_specs=[IN_SMEM] + [IN_VMEM] * 3,
        out_specs=IN_VMEM,
        compiler_params=pltpu.CompilerParams(vmem_limit_bytes=VMEM_LIMIT),
        name="project_out",
    )(place, *in_vmem(attended, w_own, w_other))


def project_kv_kernel(hid_ref, gain_ref, w_ref, out_ref):
    groups, rows, width = hid_ref.shape
    squares = jnp.zeros((rows, width), jnp.float32)
    keys = jnp.zeros((rows, width), jnp.float32)
    values = jnp.zeros((rows, width), jnp.float32)
    for group in range(groups):
        hidden = hid_ref[group].astype(jnp.float32)
        squares = squares + hidden * hidden
        scaled = (hidden * gain_ref[group : group + 1, :].astype(jnp.float32)).astype(jnp.bfloat16)
        span = slice(group * width, (group + 1) * width)
        keys = keys + jnp.dot(scaled, w_ref[0, span, :], preferred_element_type=jnp.float32)
        values = values + jnp.dot(scaled, w_ref[1, span, :], preferred_element_type=jnp.float32)
    norm = lax.rsqrt(jnp.sum(squares, axis=1, keepdims=True) / D + EPSILON)
    out_ref[0] = (keys * norm).astype(out_ref.dtype)
    out_ref[1] = (values * norm).astype(out_ref.dtype)


def project_kv(gathered, gain, w_kv, last):
    _, rows, width = gathered.shape
    shape = vmem_out((2, rows, width), jnp.float32 if last else jnp.bfloat16)
    return pl.pallas_call(
        project_kv_kernel,
        out_shape=shape,
        in_specs=[pl.BlockSpec(memory_space=pltpu.VMEM)] * 3,
        out_specs=pl.BlockSpec(memory_space=pltpu.VMEM),
        compiler_params=pltpu.CompilerParams(vmem_limit_bytes=VMEM_LIMIT),
        name="project_kv",
    )(*in_vmem(gathered, gain, w_kv))


def exchange(copies, axis):
    return lax.all_to_all(copies, axis, 0, 0, tiled=True)


def over_head(block):
    near = lax.all_gather(block, "zh", axis=0)
    return spread(near, "y", 4).reshape((16,) + block.shape)


def across(block):
    return lax.ppermute(block, "co", [(0, 1), (1, 0)])


def per_device(hidden_in, queries, kv_prev, norm_gain, w_kv, w_out):
    place = jnp.stack([lax.axis_index("zl"), lax.axis_index("x"), lax.axis_index("co")]).astype(jnp.int32)
    half = w_out.shape[0] // 2
    swap = [(zl * 4 + y, y * 4 + zl) for zl in range(4) for y in range(4)]
    w_mine = lax.ppermute(w_out, ("zl", "y"), swap)
    w_pair = jnp.transpose(w_kv, (1, 0, 2))
    gain = norm_gain.reshape(16, 256)
    block = jnp.transpose(kv_prev, (1, 0, 2))
    for iteration in range(ITERS):
        last = iteration == ITERS - 1
        line = lax.all_gather(block, "zl", axis=0)
        own = spread(line, "x", 4)
        if iteration == 0:
            w_packed = jnp.concatenate([w_mine[:half], w_mine[half:]], axis=1)
            w_line = lax.all_gather(w_packed, "zl", axis=0)
            own, w_line, w_pair = lax.optimization_barrier((own, w_line, w_pair))
            w_own = spread(w_line, "x", 4)
        other = across(own)
        state = attend(place, queries, own)
        attended = attend(place, queries, other, state)
        if iteration == 0:
            w_own, attended = lax.optimization_barrier((w_own, attended))
            w_other = across(w_own)
        attended = exchange(attended, "y")
        parts = exchange(project_out(place, attended, w_own, w_other), "zh")
        hidden = hidden_in.astype(jnp.float32) + jnp.sum(parts.astype(jnp.float32), axis=0)
        block = project_kv(over_head(hidden.astype(jnp.bfloat16)), gain, w_pair, last)
    return (hidden, jnp.transpose(block, (1, 0, 2)))


def solution(mesh):
    ctx_parts = (4, 4, 2)
    head_parts = (4, 4)
    fine = Mesh(mesh.devices.reshape(ctx_parts + head_parts), CTX + HEAD)
    in_specs = (
        P(CTX, HEAD),
        P(CTX, HEAD),
        P(CTX, None, HEAD),
        P(),
        P(None, None, HEAD),
        P(HEAD, CTX),
    )
    out_specs = (P(CTX, HEAD), P(CTX, None, HEAD))
    return jax.shard_map(per_device, mesh=fine, in_specs=in_specs, out_specs=out_specs, check_vma=False)
```

```python
import functools
import math

import jax
import jax.numpy as jnp
from jax import lax
from jax.experimental import pallas as pl
from jax.experimental.pallas import tpu as pltpu
from jax.sharding import Mesh, PartitionSpec as P


D = 4096
HD = 128
ITERS = 2

MASKED = -1e30
EPSILON = 1e-05

CTX = ("zl", "x", "co")
HEAD = ("y", "zh")
VMEM_LIMIT = 10 << 20


def spread(block, axis, count):
    copies = jnp.broadcast_to(block[None], (count,) + block.shape)
    return lax.all_to_all(copies, axis, 0, 0, tiled=True)


def in_vmem(*arrays):
    return [pltpu.with_memory_space_constraint(array, pltpu.VMEM) for array in arrays]


def vmem_out(shape, dtype):
    return pltpu.VMEM(shape, dtype)


IN_VMEM = pl.BlockSpec(memory_space=pltpu.VMEM)
IN_SMEM = pl.BlockSpec(memory_space=pltpu.SMEM)


def attend_kernel(place_ref, q_ref, kv_ref, *refs, first):
    if first:
        m_ref, l_ref, acc_ref = refs
    else:
        m_in, l_in, acc_in, out_ref = refs
    zl = place_ref[0]
    x = place_ref[1]
    co = place_ref[2]
    rows = q_ref.shape[0]
    heads = q_ref.shape[1] // HD
    factor = HD ** (-0.5) * math.log2(math.e)
    side = co if first else 1 - co
    distance = lax.broadcasted_iota(jnp.int32, (rows, 128), 0) - lax.broadcasted_iota(jnp.int32, (rows, 128), 1)
    start = zl * 1024 + x * 256 + (co - side) * 128

    for head in range(heads):
        cols = slice(head * HD, (head + 1) * HD)
        query = q_ref[:, cols]
        scores = []
        for chunk in range(4):
            keys = jnp.concatenate([kv_ref[xx, chunk, 0, :, cols] for xx in range(4)], axis=0)
            allowed = jnp.concatenate(
                [distance >= chunk * 1024 + xx * 256 - start for xx in range(4)], axis=1
            )
            product = lax.dot_general(
                query, keys, (((1,), (1,)), ((), ())), preferred_element_type=jnp.float32
            )
            scores.append(jnp.where(allowed, product, MASKED))
        peak = jnp.maximum(jnp.maximum(scores[0], scores[1]), jnp.maximum(scores[2], scores[3]))
        top = jnp.broadcast_to(jnp.max(peak, axis=1, keepdims=True), (rows, 128))
        if not first:
            before = m_in[head]
            top = jnp.maximum(before, top)
            fade = jnp.exp2((before - top) * factor)
        wide = jnp.concatenate([top] * 4, axis=1)
        weights = [jnp.exp2((piece - wide) * factor) for piece in scores]
        total = (weights[0] + weights[1]) + (weights[2] + weights[3])
        total = jnp.broadcast_to(jnp.sum(total, axis=1, keepdims=True), (rows, 128))
        mixed = None
        for chunk in range(4):
            values = jnp.concatenate([kv_ref[xx, chunk, 1, :, cols] for xx in range(4)], axis=0)
            term = jnp.dot(weights[chunk].astype(jnp.bfloat16), values, preferred_element_type=jnp.float32)
            mixed = term if mixed is None else mixed + term
        if first:
            m_ref[head] = top
            l_ref[head] = total
            acc_ref[head] = mixed
        else:
            result = ((acc_in[head] * fade + mixed) / (l_in[head] * fade + total)).astype(jnp.bfloat16)
            for copy in range(4):
                out_ref[copy, :, cols] = result


def attend(place, queries, pair, state=None):
    rows, width = queries.shape
    heads = width // HD
    kept = (heads, rows, 128)
    first = state is None
    if first:
        out_shape = [vmem_out(kept, jnp.float32)] * 3
        operands = in_vmem(queries, pair)
    else:
        out_shape = vmem_out((4, rows, width), jnp.bfloat16)
        operands = in_vmem(queries, pair, *state)
    return pl.pallas_call(
        functools.partial(attend_kernel, first=first),
        out_shape=out_shape,
        in_specs=[IN_SMEM] + [IN_VMEM] * len(operands),
        out_specs=[IN_VMEM] * 3 if first else IN_VMEM,
        compiler_params=pltpu.CompilerParams(vmem_limit_bytes=VMEM_LIMIT),
        name="attend_own" if first else "attend_other",
    )(place, *operands)


def project_out_kernel(place_ref, att_ref, w_own_ref, w_other_ref, out_ref):
    co = place_ref[2]
    for zh in range(4):
        product = None
        for y in range(4):
            block = jnp.concatenate(
                [
                    jnp.concatenate([ref[zh, y, :, :128], ref[zh, y, :, 128:]], axis=0)
                    for ref in (w_own_ref, w_other_ref)
                ],
                axis=1,
            )
            term = jnp.dot(att_ref[y], block, preferred_element_type=jnp.float32)
            product = term if product is None else product + term
        mine, theirs = product[:, :128], product[:, 128:]
        out_ref[zh, :, :128] = jnp.where(co == 0, mine, theirs).astype(jnp.bfloat16)
        out_ref[zh, :, 128:] = jnp.where(co == 0, theirs, mine).astype(jnp.bfloat16)


def project_out(place, attended, w_own, w_other):
    _, rows, width = attended.shape
    return pl.pallas_call(
        project_out_kernel,
        out_shape=vmem_out((4, rows, width), jnp.bfloat16),
        in_specs=[IN_SMEM] + [IN_VMEM] * 3,
        out_specs=IN_VMEM,
        compiler_params=pltpu.CompilerParams(vmem_limit_bytes=VMEM_LIMIT),
        name="project_out",
    )(place, *in_vmem(attended, w_own, w_other))


def project_kv_kernel(hid_ref, gain_ref, w_ref, out_ref):
    groups, rows, width = hid_ref.shape
    squares = jnp.zeros((rows, width), jnp.float32)
    keys = jnp.zeros((rows, width), jnp.float32)
    values = jnp.zeros((rows, width), jnp.float32)
    for group in range(groups):
        hidden = hid_ref[group].astype(jnp.float32)
        squares = squares + hidden * hidden
        scaled = (hidden * gain_ref[group : group + 1, :].astype(jnp.float32)).astype(jnp.bfloat16)
        span = slice(group * width, (group + 1) * width)
        keys = keys + jnp.dot(scaled, w_ref[0, span, :], preferred_element_type=jnp.float32)
        values = values + jnp.dot(scaled, w_ref[1, span, :], preferred_element_type=jnp.float32)
    norm = lax.rsqrt(jnp.sum(squares, axis=1, keepdims=True) / D + EPSILON)
    out_ref[0] = (keys * norm).astype(out_ref.dtype)
    out_ref[1] = (values * norm).astype(out_ref.dtype)


def project_kv(gathered, gain, w_kv, last):
    _, rows, width = gathered.shape
    shape = vmem_out((2, rows, width), jnp.float32 if last else jnp.bfloat16)
    return pl.pallas_call(
        project_kv_kernel,
        out_shape=shape,
        in_specs=[pl.BlockSpec(memory_space=pltpu.VMEM)] * 3,
        out_specs=pl.BlockSpec(memory_space=pltpu.VMEM),
        compiler_params=pltpu.CompilerParams(vmem_limit_bytes=VMEM_LIMIT),
        name="project_kv",
    )(*in_vmem(gathered, gain, w_kv))


def exchange(copies, axis):
    return lax.all_to_all(copies, axis, 0, 0, tiled=True)


def over_head(block):
    near = lax.all_gather(block, "zh", axis=0)
    return spread(near, "y", 4).reshape((16,) + block.shape)


def across(block):
    return lax.ppermute(block, "co", [(0, 1), (1, 0)])


def per_device(hidden_in, queries, kv_prev, norm_gain, w_kv, w_out):
    place = jnp.stack([lax.axis_index("zl"), lax.axis_index("x"), lax.axis_index("co")]).astype(jnp.int32)
    half = w_out.shape[0] // 2
    swap = [(zl * 4 + y, y * 4 + zl) for zl in range(4) for y in range(4)]
    w_mine = lax.ppermute(w_out, ("zl", "y"), swap)
    block = jnp.transpose(kv_prev, (1, 0, 2))
    for iteration in range(ITERS):
        last = iteration == ITERS - 1
        line = lax.all_gather(block, "zl", axis=0)
        own = spread(line, "x", 4)
        if iteration == 0:
            w_packed = jnp.concatenate([w_mine[:half], w_mine[half:]], axis=1)
            w_line = lax.all_gather(w_packed, "zl", axis=0)
            own, w_line, w_kv, norm_gain = lax.optimization_barrier((own, w_line, w_kv, norm_gain))
            w_pair = jnp.transpose(w_kv, (1, 0, 2))
            gain = norm_gain.reshape(16, 256)
            w_own = spread(w_line, "x", 4)
        other = across(own)
        state = attend(place, queries, own)
        attended = attend(place, queries, other, state)
        if iteration == 0:
            w_own, attended, w_pair, gain = lax.optimization_barrier((w_own, attended, w_pair, gain))
            w_other = across(w_own)
        attended = exchange(attended, "y")
        parts = exchange(project_out(place, attended, w_own, w_other), "zh")
        hidden = hidden_in.astype(jnp.float32) + jnp.sum(parts.astype(jnp.float32), axis=0)
        block = project_kv(over_head(hidden.astype(jnp.bfloat16)), gain, w_pair, last)
    return (hidden, jnp.transpose(block, (1, 0, 2)))


def solution(mesh):
    ctx_parts = (4, 4, 2)
    head_parts = (4, 4)
    fine = Mesh(mesh.devices.reshape(ctx_parts + head_parts), CTX + HEAD)
    in_specs = (
        P(CTX, HEAD),
        P(CTX, HEAD),
        P(CTX, None, HEAD),
        P(),
        P(None, None, HEAD),
        P(HEAD, CTX),
    )
    out_specs = (P(CTX, HEAD), P(CTX, None, HEAD))
    return jax.shard_map(per_device, mesh=fine, in_specs=in_specs, out_specs=out_specs, check_vma=False)
```
